32 devices in a mesh: section: 4 (over y, x), ctx: 4 (over z), tp: 2 (over core).
Axes of the slice: x: 2, y: 2, z: 4, core: 2. Of those that a mesh axis runs over, the one named last changes fastest.
Arguments:
- queries: bfloat16 [2048, 8, 8, 128], P('ctx', 'tp', 'section'), may hold values from -44 to 44
- key_states: bfloat16 [2048, 8, 128], P('ctx', 'tp'), may hold values from -4 to 4
- value_states: bfloat16 [2048, 8, 128], P('ctx', 'tp'), may hold values from -6 to 6
- out_grad: bfloat16 [2048, 8, 8, 128], P('ctx', 'tp', 'section'), may hold values from -6 to 6
- band_offsets: int32 [16, 3], replicated, may hold values from -1 to 4, as said below
- global_blocks: int32 [16, 4], replicated, may hold values from -1 to 8, as said below
Outputs:
- attended: bfloat16 [2048, 8, 8, 128], P('ctx', 'tp', 'section')
- query_grad: float32 [2048, 8, 8, 128], P('ctx', 'tp', 'section')
- key_grad: float32 [2048, 8, 128], P('ctx', 'tp')
- value_grad: float32 [2048, 8, 128], P('ctx', 'tp')
The draws below stay inside these ranges and needn't reach their ends.
Inputs may be any that keep to these rules, and one draw needn't show every extreme that they name: `band_offsets`: in every row r the first offset is 0, the second lies in 1 to 2 and the third in 3 to 4; an offset larger than r is replaced by -1. `global_blocks`: entry n of row r is either -1 or n * 4, and it is n * 4 only when n * 4 < r - 4.
All inputs are finite; a program needn't handle non-finite values.
Results may differ from the reference program's by a relative error of at most 0.017.
Values may be sent and summed in bfloat16 or wider, within the bound.
A program may use at most 128 MiB of HBM per device.

```python
import jax
import jax.numpy as jnp
from jax import lax

HD = 128
KVH = 8
GROUP = 8
BLK = 128
NBAND = 3
NGLOB = 4
L = 2048
QB_DEV = 4
NB = 16
GSTRIDE = 4


def make_keys(key):
    noise_key = jax.random.fold_in(key, 101)
    base = jnp.clip(jax.random.normal(noise_key, (L, KVH, HD), jnp.float32), -4.0, 4.0)
    return base


def draw_key_states(key, part):
    return make_keys(key).astype(jnp.bfloat16)


def draw_queries(key, part):
    base = jnp.clip(jax.random.normal(jax.random.fold_in(key, 105), (L, KVH, GROUP, HD), jnp.float32), -4.0, 4.0)
    return base.astype(jnp.bfloat16)


def draw_band_offsets(key, part):
    row_ids = jnp.arange(NB, dtype=jnp.int32)[:, None]
    half_reach = QB_DEV // 2
    second = jax.random.randint(jax.random.fold_in(key, 201), (NB, 1), 1, half_reach + 1)
    third = jax.random.randint(jax.random.fold_in(key, 202), (NB, 1), half_reach + 1, QB_DEV + 1)
    third = jnp.where(row_ids == NB - 1, QB_DEV, third)
    offsets = jnp.concatenate([jnp.zeros((NB, 1), jnp.int32), second, third], axis=1)
    return jnp.where(offsets <= row_ids, offsets, -1).astype(jnp.int32)


def draw_global_blocks(key, part):
    row_ids = jnp.arange(NB, dtype=jnp.int32)[:, None]
    blocks = jnp.arange(NGLOB, dtype=jnp.int32)[None, :] * GSTRIDE
    keeping = jax.random.randint(jax.random.fold_in(key, 301), (NB, NGLOB), 0, 4) < 3
    keeping = keeping | (row_ids == NB - 1)
    eligible = blocks < row_ids - QB_DEV
    return jnp.where(eligible & keeping, blocks, -1).astype(jnp.int32)


def level_of(own_key, shape, split, low, top_value):
    factor_of = 1.0
    for dim, shards_of in split:
        steps = jax.random.uniform(jax.random.fold_in(jax.random.fold_in(own_key, 6), dim), (shards_of,), jnp.float32, low / len(split), top_value / len(split))
        factor_of = factor_of * jnp.repeat(jnp.exp(steps), shape[dim] // shards_of).reshape((-1,) + (1,) * (len(shape) - 1 - dim))
    return factor_of


def normal_values(stream_key, dims, deviation, bound, cuts=(), held_as=jnp.bfloat16):
    result = jax.random.normal(stream_key, dims, jnp.float32) * deviation
    if len(cuts) > 0:
        result = level_of(stream_key, dims, cuts, -0.22, 0.18) * result
    return jnp.clip(result, min=-bound, max=bound).astype(held_as)


def setup_inputs(seed: int = 0) -> dict:
    keys = jax.random.split(jax.random.key(seed), 7)
    return {
        "queries": draw_queries(jax.random.fold_in(keys[6], 71), 0),
        "key_states": draw_key_states(jax.random.fold_in(keys[6], 71), 0),
        "value_states": normal_values(keys[2], (L, KVH, HD), 1.0, 6.0, ((0, 4), (1, 2))),
        "out_grad": normal_values(keys[3], (L, KVH, GROUP, HD), 1.0, 6.0, ((0, 4), (1, 2), (2, 4))),
        "band_offsets": draw_band_offsets(jax.random.fold_in(keys[6], 71), 0),
        "global_blocks": draw_global_blocks(jax.random.fold_in(keys[6], 71), 0),
    }


def block_lists(band_offsets, global_blocks):
    row_ids = jnp.arange(band_offsets.shape[0], dtype=jnp.int32)[:, None]
    band_ids = row_ids - band_offsets
    chosen = jnp.concatenate([band_ids, global_blocks], axis=1)
    usable = jnp.concatenate([band_offsets >= 0, global_blocks >= 0], axis=1)
    return jnp.where(usable, chosen, 0).astype(jnp.int32), usable


def reference(queries, key_states, value_states, out_grad, band_offsets, global_blocks):
    scale_factor = HD ** -0.5
    block_ids, usable = block_lists(band_offsets, global_blocks)
    query_blocks = queries.reshape(NB, BLK, KVH, GROUP, HD)
    grad_blocks = out_grad.reshape(NB, BLK, KVH, GROUP, HD)
    key_blocks = key_states.reshape(NB, BLK, KVH, HD)
    value_blocks = value_states.reshape(NB, BLK, KVH, HD)
    lower_half = jnp.arange(BLK)[:, None] >= jnp.arange(BLK)[None, :]
    first_slot = jnp.arange(NBAND + NGLOB) == 0

    def step_row(running, inputs):
        key_acc, value_acc = running
        row_ids, row_ok, query_row, grad_row = inputs
        key_sel = key_blocks[row_ids].astype(jnp.float32)
        value_sel = value_blocks[row_ids].astype(jnp.float32)
        query_wide = query_row.astype(jnp.float32)
        grad_wide = grad_row.astype(jnp.float32)
        scores = jnp.einsum('ihgd,njhd->hginj', query_wide, key_sel) * scale_factor
        reach = jnp.logical_not(first_slot)[None, :, None] | lower_half[:, None, :]
        allowed = row_ok[None, :, None] & reach
        scores = jnp.where(allowed, scores, -jnp.inf)
        row_top = jnp.max(scores, axis=(3, 4), keepdims=True)
        row_total = jnp.sum(jnp.exp(scores - row_top), axis=(3, 4), keepdims=True)
        log_total = row_top + jnp.log(row_total)
        weights = jnp.exp(scores - log_total)
        weights_low = weights.astype(jnp.bfloat16)
        low_wide = weights_low.astype(jnp.float32)
        attended = jnp.einsum('hginj,njhd->ihgd', low_wide, value_sel).astype(jnp.bfloat16)
        row_dots = jnp.sum(grad_wide * attended.astype(jnp.float32), axis=-1)
        dweights = jnp.einsum('ihgd,njhd->hginj', grad_wide, value_sel)
        dscores = (weights * (dweights - jnp.transpose(row_dots, (1, 2, 0))[..., None, None])).astype(jnp.bfloat16)
        dscore_wide = dscores.astype(jnp.float32)
        query_grad = scale_factor * jnp.einsum('hginj,njhd->ihgd', dscore_wide, key_sel)
        key_part = scale_factor * jnp.einsum('hginj,ihgd->njhd', dscore_wide, query_wide)
        value_part = jnp.einsum('hginj,ihgd->njhd', low_wide, grad_wide)
        key_acc = key_acc.at[row_ids].add(key_part)
        value_acc = value_acc.at[row_ids].add(value_part)
        return (key_acc, value_acc), (attended, query_grad)

    empty_grads = jnp.zeros((NB, BLK, KVH, HD), jnp.float32)
    (key_acc, value_acc), (attended, query_grad) = lax.scan(
        step_row, (empty_grads, empty_grads), (block_ids, usable, query_blocks, grad_blocks))
    return (attended.reshape(L, KVH, GROUP, HD), query_grad.reshape(L, KVH, GROUP, HD),
            key_acc.reshape(L, KVH, HD), value_acc.reshape(L, KVH, HD))
```

```python
import functools

import jax
import jax.numpy as jnp
from jax import lax
from jax.experimental import pallas as pl
from jax.experimental.pallas import tpu as pltpu
from jax.sharding import PartitionSpec as P

BLK = 128
NBAND = 3
NGLOB = 4
REACH = ((1, 2), (3, 4))
LOG2E = 1.4426950408889634
LOW = -1e30


def global_count(all_blocks, stride_blocks, own_blocks):
    return len([n for n in range(NGLOB) if n * stride_blocks < all_blocks - 1 - own_blocks])


def dot_nt(a, b):
    return lax.dot_general(a, b, (((1,), (1,)), ((), ())), preferred_element_type=jnp.float32)


def dot_tn(a, b):
    return lax.dot_general(a, b, (((0,), (0,)), ((), ())), preferred_element_type=jnp.float32)


def dot_nn(a, b):
    return lax.dot_general(a, b, (((1,), (0,)), ((), ())), preferred_element_type=jnp.float32)


def head_rows(own_blocks, n_glob, scale, row_base, band_ref, glob_ref, q_of, g_of, key_of, value_of,
              put_att, put_dq, add_key, add_value):
    for i in range(own_blocks):
        row = row_base + i
        offs = [band_ref[row, 1 + m] for m in range(NBAND - 1)]
        chosen = [glob_ref[row, n] for n in range(n_glob)]
        q, g = q_of(i), g_of(i)

        def selected(block_of):
            parts = [block_of(own_blocks + i)]
            for m in range(NBAND - 1):
                near, far = REACH[m]
                parts.append(jnp.where(offs[m] == near, block_of(own_blocks + i - near),
                                       block_of(own_blocks + i - far)))
            for n in range(n_glob):
                parts.append(block_of(2 * own_blocks + n))
            return jnp.concatenate(parts, axis=0)

        keys, values = selected(key_of), selected(value_of)
        scores = dot_nt(keys, q)
        width = scores.shape[1]
        key_pos = lax.broadcasted_iota(jnp.int32, (BLK, width), 0)
        query_pos = lax.broadcasted_iota(jnp.int32, (BLK, width), 1) % BLK
        usable = [o >= 0 for o in offs] + [c >= 0 for c in chosen]
        pieces = [jnp.where(key_pos <= query_pos, scores[:BLK], LOW)]
        for n, ok in enumerate(usable):
            pieces.append(scores[(n + 1) * BLK:(n + 2) * BLK] + jnp.where(ok, 0.0, LOW))
        scores = jnp.concatenate(pieces, axis=0)
        top = jnp.max(scores, axis=0, keepdims=True)
        probs = jnp.exp2((scores - top) * (scale * LOG2E))
        weights = probs * (1.0 / jnp.sum(probs, axis=0, keepdims=True))
        low = weights.astype(jnp.bfloat16)
        att = dot_tn(values, low).astype(jnp.bfloat16).astype(jnp.float32)
        put_att(i, att.T.astype(jnp.bfloat16))
        dots = jnp.sum(g.astype(jnp.float32).T * att, axis=0, keepdims=True)
        ds = (weights * (dot_nt(values, g) - dots)).astype(jnp.bfloat16)
        put_dq(i, (dot_tn(keys, ds) * scale).T)
        dk, dv = dot_nn(ds, q) * scale, dot_nn(low, g)
        for part, add in ((dk, add_key), (dv, add_value)):
            add(own_blocks + i, part[:BLK])
            for m in range(NBAND - 1):
                piece = part[(m + 1) * BLK:(m + 2) * BLK]
                for off in REACH[m]:
                    add(own_blocks + i - off, jnp.where(offs[m] == off, piece, 0.0))
            for n in range(n_glob):
                at = (NBAND + n) * BLK
                add(2 * own_blocks + n, part[at:at + BLK])


def local_kernel(own_blocks, n_glob, scale, band_ref, glob_ref, q_ref, g_ref, kv_ref, att_ref, dq_ref, grads_ref,
                 acc_ref):
    row_base = lax.axis_index("ctx") * own_blocks
    touched = set()

    def add_to(which):
        def add(slot, part):
            if (which, slot) in touched:
                acc_ref[which, slot] += part
            else:
                acc_ref[which, slot] = part
                touched.add((which, slot))
        return add

    def put_att(i, x):
        att_ref[0, i] = x

    def put_dq(i, x):
        dq_ref[0, i] = x

    head_rows(own_blocks, n_glob, scale, row_base, band_ref, glob_ref,
              lambda i: q_ref[0, i], lambda i: g_ref[0, i],
              lambda slot: kv_ref[0, 0, slot], lambda slot: kv_ref[1, 0, slot],
              put_att, put_dq, add_to(0), add_to(1))
    grads_ref[:, 0] = acc_ref[...].astype(grads_ref.dtype)


def passed_along(shard, axis, by):
    count = lax.axis_size(axis)
    pairs = [(i, i + by) for i in range(count) if 0 <= i + by < count]
    return lax.ppermute(shard, axis, pairs)


def rows_first(x, own_blocks):
    tok, heads, group, dim = x.shape
    x = x.reshape(own_blocks, BLK, heads, group, dim)
    return jnp.transpose(x, (2, 0, 3, 1, 4)).reshape(heads, own_blocks, group * BLK, dim)


def rows_back(x, group):
    heads, own_blocks, _, dim = x.shape
    x = x.reshape(heads, own_blocks, group, BLK, dim)
    return jnp.transpose(x, (1, 3, 0, 2, 4)).reshape(own_blocks * BLK, heads, group, dim)


def shards(queries, key_states, value_states, out_grad, band_offsets, global_blocks):
    tok, heads, group, dim = queries.shape
    own_blocks = tok // BLK
    ctx_count = lax.axis_size("ctx")
    all_blocks = own_blocks * ctx_count
    stride_blocks = all_blocks // NGLOB
    stride_devices = stride_blocks // own_blocks
    n_glob = global_count(all_blocks, stride_blocks, own_blocks)
    position = lax.axis_index("ctx")
    scale = dim ** (-0.5)
    q, g = rows_first(queries, own_blocks), rows_first(out_grad, own_blocks)
    own = jnp.stack([key_states, value_states]).transpose(0, 2, 1, 3).reshape(2, heads, own_blocks, BLK, dim)
    earlier = passed_along(own, "ctx", 1)
    firsts = lax.all_gather(own[:, :, 0], "ctx", axis=2)[:, :, ::stride_devices][:, :, :n_glob]
    stacked = jnp.concatenate([earlier, own, firsts], axis=2)
    slots = 2 * own_blocks + n_glob
    smem = pl.BlockSpec(memory_space=pltpu.SMEM)
    row_spec = pl.BlockSpec((1, own_blocks, group * BLK, dim), lambda h: (h, 0, 0, 0))
    slot_spec = pl.BlockSpec((2, 1, slots, BLK, dim), lambda h: (0, h, 0, 0, 0))
    att, dq, grads = pl.pallas_call(
        functools.partial(local_kernel, own_blocks, n_glob, scale),
        grid=(heads,),
        in_specs=[smem, smem, row_spec, row_spec, slot_spec],
        out_specs=[row_spec, row_spec, slot_spec],
        out_shape=[
            jax.ShapeDtypeStruct(q.shape, jnp.bfloat16),
            jax.ShapeDtypeStruct(q.shape, jnp.float32),
            jax.ShapeDtypeStruct((2, heads, slots, BLK, dim), jnp.bfloat16),
        ],
        scratch_shapes=[pltpu.VMEM((2, slots, BLK, dim), jnp.float32)],
        compiler_params=pltpu.CompilerParams(vmem_limit_bytes=56 * 2**20),
    )(band_offsets, global_blocks, q, g, stacked)
    back = passed_along(grads[:, :, :own_blocks], "ctx", -1)
    own_grads = grads[:, :, own_blocks:2 * own_blocks].astype(jnp.float32) + back.astype(jnp.float32)
    summed = lax.psum(grads[:, :, 2 * own_blocks:], "ctx").astype(jnp.float32)
    mine = (jnp.arange(n_glob) * stride_devices == position)[None, None, :, None, None]
    first = jnp.sum(jnp.where(mine, summed, 0.0), axis=2)
    own_grads = jnp.concatenate([own_grads[:, :, :1] + first[:, :, None], own_grads[:, :, 1:]], axis=2)
    totals = lax.psum(own_grads.astype(jnp.bfloat16), "section").astype(jnp.float32)
    totals = totals.reshape(2, heads, tok, dim).transpose(0, 2, 1, 3)
    return rows_back(att, group), rows_back(dq, group), totals[0], totals[1]


def solution(mesh):
    wide, narrow = P("ctx", "tp", "section", None), P("ctx", "tp", None)
    return jax.shard_map(
        shards,
        mesh=mesh,
        in_specs=(wide, narrow, narrow, wide, P(), P()),
        out_specs=(wide, wide, narrow, narrow),
        check_vma=False,
    )
```

```python
import functools

import jax
import jax.numpy as jnp
from jax import lax
from jax.experimental import pallas as pl
from jax.experimental.pallas import tpu as pltpu
from jax.sharding import PartitionSpec as P

BLK = 128
NBAND = 3
NGLOB = 4
REACH = ((1, 2), (3, 4))
LOG2E = 1.4426950408889634
LOW = -1e30


def global_count(all_blocks, stride_blocks, own_blocks):
    return len([n for n in range(NGLOB) if n * stride_blocks < all_blocks - 1 - own_blocks])


def dot_nt(a, b):
    return lax.dot_general(a, b, (((1,), (1,)), ((), ())), preferred_element_type=jnp.float32)


def dot_tn(a, b):
    return lax.dot_general(a, b, (((0,), (0,)), ((), ())), preferred_element_type=jnp.float32)


def dot_nn(a, b):
    return lax.dot_general(a, b, (((1,), (0,)), ((), ())), preferred_element_type=jnp.float32)


def head_rows(own_blocks, n_glob, scale, row_base, band_ref, glob_ref, q_of, g_of, key_of, value_of,
              put_att, put_dq, add_key, add_value, rows):
    for i in rows:
        row = row_base + i
        offs = [band_ref[row, 1 + m] for m in range(NBAND - 1)]
        chosen = [glob_ref[row, n] for n in range(n_glob)]
        q, g = q_of(i), g_of(i)

        def selected(block_of):
            parts = [block_of(own_blocks + i)]
            for m in range(NBAND - 1):
                near, far = REACH[m]
                parts.append(jnp.where(offs[m] == near, block_of(own_blocks + i - near),
                                       block_of(own_blocks + i - far)))
            for n in range(n_glob):
                parts.append(block_of(2 * own_blocks + n))
            return jnp.concatenate(parts, axis=0)

        keys, values = selected(key_of), selected(value_of)
        scores = dot_nt(keys, q)
        width = scores.shape[1]
        key_pos = lax.broadcasted_iota(jnp.int32, (BLK, width), 0)
        query_pos = lax.broadcasted_iota(jnp.int32, (BLK, width), 1) % BLK
        usable = [o >= 0 for o in offs] + [c >= 0 for c in chosen]
        pieces = [jnp.where(key_pos <= query_pos, scores[:BLK], LOW)]
        for n, ok in enumerate(usable):
            pieces.append(scores[(n + 1) * BLK:(n + 2) * BLK] + jnp.where(ok, 0.0, LOW))
        scores = jnp.concatenate(pieces, axis=0)
        top = jnp.max(scores, axis=0, keepdims=True)
        probs = jnp.exp2((scores - top) * (scale * LOG2E))
        weights = probs * (1.0 / jnp.sum(probs, axis=0, keepdims=True))
        low = weights.astype(jnp.bfloat16)
        att = dot_tn(values, low).astype(jnp.bfloat16).astype(jnp.float32)
        put_att(i, att.T.astype(jnp.bfloat16))
        dots = jnp.sum(g.astype(jnp.float32).T * att, axis=0, keepdims=True)
        ds = (weights * (dot_nt(values, g) - dots)).astype(jnp.bfloat16)
        put_dq(i, (dot_tn(keys, ds) * scale).T)
        dk, dv = dot_nn(ds, q) * scale, dot_nn(low, g)
        for part, add in ((dk, add_key), (dv, add_value)):
            add(own_blocks + i, part[:BLK])
            for m in range(NBAND - 1):
                piece = part[(m + 1) * BLK:(m + 2) * BLK]
                for off in REACH[m]:
                    add(own_blocks + i - off, jnp.where(offs[m] == off, piece, 0.0))
            for n in range(n_glob):
                at = (NBAND + n) * BLK
                add(2 * own_blocks + n, part[at:at + BLK])


def fused_kernel(own, n_glob, owner_step, ctx_count, bits, scale, band_ref, glob_ref, q_ref, g_ref, kv_ref,
                 att_ref, dq_ref, out_ref,
                 seen, acc, acc_own, parts, paired, halves, returned, farback, totals, swapped,
                 near_s, near_r, far_s, far_r, pair_s, pair_r, farpair_s, farpair_r,
                 one_s, one_r, farone_s, farone_r, back_s, back_r, farback_s, farback_r,
                 two_s, two_r, three_s, three_r):
    heads = kv_ref.shape[1]
    p, s, parity = lax.axis_index("ctx"), lax.axis_index("section"), lax.axis_index("tp") % 2

    def other(j):
        bit = (1 << (j % bits)) * (1 - parity) + (1 << ((j + 1) % bits)) * parity
        side = (s // bit) % 2
        return s + bit * (1 - 2 * side), side

    mate, role = other(0)
    has_prev, has_next = p > 0, p < ctx_count - 1
    index = p // owner_step

    def owns(at):
        return jnp.logical_and(at % owner_step == 0, at // owner_step < n_glob)

    def sends_far(d):
        return jnp.logical_and(owns(p), p + d < ctx_count)

    def gets_far(d):
        return jnp.logical_and(p - d >= 0, owns(p - d + (p - d < 0) * ctx_count * owner_step))

    spans = range(2, ctx_count)

    def is_far(n):
        return p >= n * owner_step + 2

    def is_next(n):
        return p == n * owner_step + 1

    def copy(src, dst, ss, rs, axis, to):
        return pltpu.make_async_remote_copy(src_ref=src, dst_ref=dst, send_sem=ss, recv_sem=rs,
                                            device_id={axis: to}, device_id_type=pl.DeviceIdType.MESH)

    bar = pltpu.get_barrier_semaphore()
    links = [(has_prev, "ctx", p - 1), (has_next, "ctx", p + 1)]
    for d in spans:
        links += [(sends_far(d), "ctx", p + d), (gets_far(d), "ctx", p - d)]
    for j in range(bits):
        pl.semaphore_signal(bar, inc=1, device_id={"section": other(j)[0]}, device_id_type=pl.DeviceIdType.MESH)
    for cond, axis, to in links:
        @pl.when(cond)
        def _(axis=axis, to=to):
            pl.semaphore_signal(bar, inc=1, device_id={axis: to}, device_id_type=pl.DeviceIdType.MESH)
    peers = bits
    for cond, _, _ in links:
        peers = peers + jnp.where(cond, 1, 0)
    pl.semaphore_wait(bar, peers)

    def near_copy(h):
        return copy(kv_ref.at[role, h], seen.at[role, h, pl.ds(0, own)], near_s.at[h], near_r.at[h], "ctx", p + 1)

    def far_copy(h, d):
        return copy(kv_ref.at[role, h, 0], seen.at[role, h, own + index], far_s.at[h, d], far_r.at[h, index],
                    "ctx", p + d)

    def far_arrival(h, n):
        return copy(kv_ref.at[role, h, 0], seen.at[role, h, own + n], far_s.at[h, 0], far_r.at[h, n], "ctx", p)

    def pair_copy(h, half):
        blocks = seen.at[half, h, pl.ds(0, own)]
        return copy(blocks, blocks, pair_s.at[h], pair_r.at[h], "section", mate)

    def farpair_copy(h, n, half):
        block = seen.at[half, h, own + n]
        return copy(block, block, farpair_s.at[h, n], farpair_r.at[h, n], "section", mate)

    def one_copy(h, src_half):
        return copy(parts.at[src_half, h, pl.ds(0, 2 * own)], paired.at[h, pl.ds(0, 2 * own)],
                    one_s.at[h], one_r.at[h], "section", mate)

    def farone_copy(h, n, src_half):
        return copy(parts.at[src_half, h, 2 * own + n], paired.at[h, 2 * own + n],
                    farone_s.at[h, n], farone_r.at[h, n], "section", mate)

    def back_copy(h):
        return copy(halves.at[h, pl.ds(0, own)], returned.at[h], back_s.at[h], back_r.at[h], "ctx", p - 1)

    def farback_copy(h, n):
        return copy(halves.at[h, 2 * own + n], farback.at[h, p - n * owner_step], farback_s.at[h, n],
                    farback_r.at[h, p - n * owner_step], "ctx", n * owner_step)

    def farback_arrival(h, d):
        return copy(halves.at[h, 2 * own], farback.at[h, d], farback_s.at[h, 0], farback_r.at[h, d], "ctx", p)

    def two_copy(h, j):
        return copy(totals.at[j, h], swapped.at[j, h], two_s.at[j, h], two_r.at[j, h], "section", other(j)[0])

    def three_copy(h, half):
        return copy(out_ref.at[half, h], out_ref.at[half, h], three_s.at[h], three_r.at[h], "section", mate)

    for h in range(heads):
        @pl.when(has_next)
        def _(h=h):
            near_copy(h).start()
        for d in spans:
            @pl.when(sends_far(d))
            def _(h=h, d=d):
                far_copy(h, d).start()

    @pl.when(jnp.logical_not(has_prev))
    def _():
        seen[:, :, :own] = jnp.zeros_like(seen[:, :, :own])
    for n in range(n_glob):
        @pl.when(p < n * owner_step + 1)
        def _(n=n):
            seen[:, :, own + n] = jnp.zeros_like(seen[:, :, own + n])

    def pass_on(h):
        @pl.when(has_prev)
        def _():
            near_copy(h).wait_recv()
            pair_copy(h, role).start()
        for n in range(n_glob):
            @pl.when(is_far(n))
            def _(n=n):
                far_arrival(h, n).wait_recv()
                farpair_copy(h, n, role).start()

    def arrived(h):
        @pl.when(has_prev)
        def _():
            pair_copy(h, 1 - role).wait_recv()
        for n in range(n_glob):
            @pl.when(is_far(n))
            def _(n=n):
                farpair_copy(h, n, 1 - role).wait_recv()

            @pl.when(is_next(n))
            def _(n=n):
                seen[:, h, own + n] = seen[:, h, 0]

    touched = set()

    def add_to(which):
        def add(slot, part):
            if (which, slot) in touched:
                acc[which, slot] += part
            else:
                acc[which, slot] = part
                touched.add((which, slot))
        return add

    def block_of(which, h):
        def get(slot):
            if slot < own:
                return seen[which, h, slot]
            if slot < 2 * own:
                return kv_ref[which, h, slot - own]
            return seen[which, h, slot - own]
        return get

    def compute(h, rows):
        def put_att(i, x):
            att_ref[h, i] = x

        def put_dq(i, x):
            dq_ref[h, i] = x

        head_rows(own, n_glob, scale, p * own, band_ref, glob_ref, lambda i: q_ref[h, i], lambda i: g_ref[h, i],
                  block_of(0, h), block_of(1, h), put_att, put_dq, add_to(0), add_to(1), rows)

    def send_parts(h):
        for n in range(n_glob):
            @pl.when(is_next(n))
            def _(n=n):
                acc[:, 0] += acc[:, 2 * own + n]
        parts[:, h] = acc[...].astype(parts.dtype)
        one_copy(h, 1 - role).start()
        for n in range(n_glob):
            @pl.when(is_far(n))
            def _(n=n):
                farone_copy(h, n, 1 - role).start()

    def wide(x):
        return x.astype(jnp.float32)

    def send_back(h):
        one_copy(h, role).wait_recv()
        both = pl.ds(0, 2 * own)
        halves[h, both] = (wide(parts[role, h, both]) + wide(paired[h, both])).astype(halves.dtype)

        @pl.when(has_prev)
        def _():
            back_copy(h).start()
        for n in range(n_glob):
            @pl.when(is_far(n))
            def _(n=n):
                farone_copy(h, n, role).wait_recv()
                at = 2 * own + n
                halves[h, at] = (wide(parts[role, h, at]) + wide(paired[h, at])).astype(halves.dtype)
                farback_copy(h, n).start()

    def swap(h):
        mine = pl.ds(own, own)
        total = acc_own
        total[...] = wide(halves[h, mine])

        @pl.when(has_next)
        def _():
            back_copy(h).wait_recv()
            total[...] += wide(returned[h])
        for d in spans:
            @pl.when(sends_far(d))
            def _(d=d):
                farback_arrival(h, d).wait_recv()
                total[0] += wide(farback[h, d])
        totals[1, h] = total[...].astype(totals.dtype)
        two_copy(h, 1).start()

    def spread(h):
        for j in range(1, bits):
            two_copy(h, j).wait_recv()
            result = (wide(totals[j, h]) + wide(swapped[j, h])).astype(totals.dtype)
            if j + 1 < bits:
                totals[j + 1, h] = result
                two_copy(h, j + 1).start()
            else:
                out_ref[role, h] = result
        three_copy(h, role).start()

    pass_on(0)

    def step(h, carry):
        @pl.when(h + 1 < heads)
        def _():
            pass_on(h + 1)

        @pl.when(h >= 3)
        def _():
            spread(h - 3)

        @pl.when(jnp.logical_and(h >= 2, h < heads + 2))
        def _():
            swap(h - 2)

        @pl.when(h < heads)
        def _():
            arrived(h)
            compute(h, range(own // 2))

        @pl.when(jnp.logical_and(h >= 1, h < heads + 1))
        def _():
            send_back(h - 1)

        @pl.when(h < heads)
        def _():
            compute(h, range(own // 2, own))
            send_parts(h)
        return carry

    lax.fori_loop(0, heads + 3, step, 0)

    def finish(h, carry):
        @pl.when(has_next)
        def _():
            near_copy(h).wait_send()
        for d in spans:
            @pl.when(sends_far(d))
            def _(d=d):
                far_copy(h, d).wait_send()

        @pl.when(has_prev)
        def _():
            pair_copy(h, role).wait_send()
            back_copy(h).wait_send()
        one_copy(h, 1 - role).wait_send()
        for n in range(n_glob):
            @pl.when(is_far(n))
            def _(n=n):
                farpair_copy(h, n, role).wait_send()
                farone_copy(h, n, 1 - role).wait_send()
                farback_copy(h, n).wait_send()
        for j in range(1, bits):
            two_copy(h, j).wait_send()
        three_copy(h, role).wait_send()
        three_copy(h, 1 - role).wait_recv()
        return carry

    lax.fori_loop(0, heads, finish, 0)


def rows_first(x, own_blocks):
    tok, heads, group, dim = x.shape
    x = x.reshape(own_blocks, BLK, heads, group, dim)
    return jnp.transpose(x, (2, 0, 3, 1, 4)).reshape(heads, own_blocks, group * BLK, dim)


def rows_back(x, group):
    heads, own_blocks, _, dim = x.shape
    x = x.reshape(heads, own_blocks, group, BLK, dim)
    return jnp.transpose(x, (1, 3, 0, 2, 4)).reshape(own_blocks * BLK, heads, group, dim)


def shards(queries, key_states, value_states, out_grad, band_offsets, global_blocks):
    tok, heads, group, dim = queries.shape
    own = tok // BLK
    ctx_count, sections = lax.axis_size("ctx"), lax.axis_size("section")
    bits = sections.bit_length() - 1
    all_blocks = own * ctx_count
    stride_blocks = all_blocks // NGLOB
    n_glob = global_count(all_blocks, stride_blocks, own)
    slots = 2 * own + n_glob
    q, g = rows_first(queries, own), rows_first(out_grad, own)
    kv = jnp.stack([key_states, value_states]).transpose(0, 2, 1, 3).reshape(2, heads, own, BLK, dim)
    smem, vmem = pl.BlockSpec(memory_space=pltpu.SMEM), pl.BlockSpec(memory_space=pltpu.VMEM)

    def low(*lead):
        return pltpu.VMEM((*lead, BLK, dim), jnp.bfloat16)

    def sems(*dims):
        return [pltpu.SemaphoreType.DMA(dims)] * 2

    att, dq, totals = pl.pallas_call(
        functools.partial(fused_kernel, own, n_glob, stride_blocks // own, ctx_count, bits, dim ** (-0.5)),
        in_specs=[smem, smem, vmem, vmem, vmem],
        out_specs=[vmem, vmem, vmem],
        out_shape=[
            jax.ShapeDtypeStruct(q.shape, jnp.bfloat16),
            jax.ShapeDtypeStruct(q.shape, jnp.float32),
            jax.ShapeDtypeStruct(kv.shape, jnp.bfloat16),
        ],
        scratch_shapes=[
            low(2, heads, own + n_glob),
            pltpu.VMEM((2, slots, BLK, dim), jnp.float32),
            pltpu.VMEM((own, BLK, dim), jnp.float32),
            low(2, heads, slots), low(heads, slots), low(heads, slots), low(heads, own), low(heads, ctx_count),
            low(bits, heads, own), low(bits, heads, own),
            *sems(heads), pltpu.SemaphoreType.DMA((heads, ctx_count)), pltpu.SemaphoreType.DMA((heads, n_glob)),
            *sems(heads), *sems(heads, n_glob),
            *sems(heads), *sems(heads, n_glob),
            *sems(heads), pltpu.SemaphoreType.DMA((heads, n_glob)), pltpu.SemaphoreType.DMA((heads, ctx_count)),
            *sems(bits, heads), *sems(heads),
        ],
        compiler_params=pltpu.CompilerParams(
            vmem_limit_bytes=56 * 2**20, collective_id=0, has_side_effects=True),
    )(band_offsets, global_blocks, q, g, kv)
    totals = totals.reshape(2, heads, tok, dim).transpose(0, 2, 1, 3).astype(jnp.float32)
    return rows_back(att, group), rows_back(dq, group), totals[0], totals[1]


def solution(mesh):
    wide, narrow = P("ctx", "tp", "section", None), P("ctx", "tp", None)
    return jax.shard_map(
        shards,
        mesh=mesh,
        in_specs=(wide, narrow, narrow, wide, P(), P()),
        out_specs=(wide, wide, narrow, narrow),
        check_vma=False,
    )
```

```python
import functools

import jax
import jax.numpy as jnp
from jax import lax
from jax.experimental import pallas as pl
from jax.experimental.pallas import tpu as pltpu
from jax.sharding import PartitionSpec as P

BLK = 128
NBAND = 3
NGLOB = 4
REACH = ((1, 2), (3, 4))
LOG2E = 1.4426950408889634
LOW = -1e30


def global_count(all_blocks, stride_blocks, own_blocks):
    return len([n for n in range(NGLOB) if n * stride_blocks < all_blocks - 1 - own_blocks])


def dot_nt(a, b):
    return lax.dot_general(a, b, (((1,), (1,)), ((), ())), preferred_element_type=jnp.float32)


def dot_tn(a, b):
    return lax.dot_general(a, b, (((0,), (0,)), ((), ())), preferred_element_type=jnp.float32)


def dot_nn(a, b):
    return lax.dot_general(a, b, (((1,), (0,)), ((), ())), preferred_element_type=jnp.float32)


def head_rows(own_blocks, n_glob, scale, row_base, band_ref, glob_ref, q_of, g_of, key_of, value_of,
              put_att, put_dq, add_key, add_value, rows):
    for i in rows:
        row = row_base + i
        offs = [band_ref[1 + m, row] for m in range(NBAND - 1)]
        chosen = [glob_ref[n, row] for n in range(n_glob)]
        q, g = q_of(i), g_of(i)

        def selected(block_of):
            parts = [block_of(own_blocks + i)]
            for m in range(NBAND - 1):
                near, far = REACH[m]
                parts.append(jnp.where(offs[m] == near, block_of(own_blocks + i - near),
                                       block_of(own_blocks + i - far)))
            for n in range(n_glob):
                parts.append(block_of(2 * own_blocks + n))
            return jnp.concatenate(parts, axis=0)

        keys, values = selected(key_of), selected(value_of)
        scores = dot_nt(keys, q)
        width = scores.shape[1]
        key_pos = lax.broadcasted_iota(jnp.int32, (BLK, width), 0)
        query_pos = lax.broadcasted_iota(jnp.int32, (BLK, width), 1) % BLK
        usable = [o >= 0 for o in offs] + [c >= 0 for c in chosen]
        pieces = [jnp.where(key_pos <= query_pos, scores[:BLK], LOW)]
        for n, ok in enumerate(usable):
            pieces.append(scores[(n + 1) * BLK:(n + 2) * BLK] + jnp.where(ok, 0.0, LOW))
        scores = jnp.concatenate(pieces, axis=0)
        top = jnp.max(scores, axis=0, keepdims=True)
        probs = jnp.exp2((scores - top) * (scale * LOG2E))
        weights = probs * (1.0 / jnp.sum(probs, axis=0, keepdims=True))
        low = weights.astype(jnp.bfloat16)
        att = dot_tn(values, low).astype(jnp.bfloat16).astype(jnp.float32)
        put_att(i, att.T)
        dots = jnp.sum(g.astype(jnp.float32).T * att, axis=0, keepdims=True)
        ds = (weights * (dot_nt(values, g) - dots)).astype(jnp.bfloat16)
        put_dq(i, (dot_tn(keys, ds) * scale).T)
        dk, dv = dot_nn(ds, q) * scale, dot_nn(low, g)
        for part, add in ((dk, add_key), (dv, add_value)):
            add(own_blocks + i, part[:BLK])
            for m in range(NBAND - 1):
                piece = part[(m + 1) * BLK:(m + 2) * BLK]
                for off in REACH[m]:
                    add(own_blocks + i - off, jnp.where(offs[m] == off, piece, 0.0))
            for n in range(n_glob):
                at = (NBAND + n) * BLK
                add(2 * own_blocks + n, part[at:at + BLK])


def fused_kernel(own, n_glob, owner_step, ctx_count, bits, scale, group, band_ref, glob_ref, q_ref, g_ref,
                 key_ref, value_ref, att_ref, dq_ref, dkey_ref, dvalue_ref,
                 kv_wide, kv_ref, q_wide, g_wide, att_wide, out_ref, seen, acc, acc_own, parts, paired, halves, returned, farback, totals, swapped,
                 near_s, near_r, far_s, far_r, pair_s, pair_r, farpair_s, farpair_r,
                 one_s, one_r, own_s, own_r, farone_s, farone_r, back_s, back_r, farback_s, farback_r,
                 two_s, two_r, three_s, three_r):
    heads, dim = kv_ref.shape[1], kv_ref.shape[-1]
    tok, lanes = own * BLK, heads * group

    for which, ref in enumerate((key_ref, value_ref)):
        kv_wide[...] = ref[...].astype(jnp.float32)
        for h in range(heads):
            kv_ref[which, h] = kv_wide[pl.ds(h, tok, stride=heads), :].astype(kv_ref.dtype).reshape(own, BLK, dim)
    p, s, parity = lax.axis_index("ctx"), lax.axis_index("section"), lax.axis_index("tp") % 2

    def other(j):
        bit = (1 << (j % bits)) * (1 - parity) + (1 << ((j + 1) % bits)) * parity
        side = (s // bit) % 2
        return s + bit * (1 - 2 * side), side

    mate, role = other(0)
    has_prev, has_next = p > 0, p < ctx_count - 1
    index = p // owner_step

    def owns(at):
        return jnp.logical_and(at % owner_step == 0, at // owner_step < n_glob)

    def sends_far(d):
        return jnp.logical_and(owns(p), p + d < ctx_count)

    def gets_far(d):
        return jnp.logical_and(p - d >= 0, owns(p - d + (p - d < 0) * ctx_count * owner_step))

    spans = range(2, ctx_count)

    def is_far(n):
        return p >= n * owner_step + 2

    def is_next(n):
        return p == n * owner_step + 1

    def copy(src, dst, ss, rs, axis, to):
        return pltpu.make_async_remote_copy(src_ref=src, dst_ref=dst, send_sem=ss, recv_sem=rs,
                                            device_id={axis: to}, device_id_type=pl.DeviceIdType.MESH)

    bar = pltpu.get_barrier_semaphore()
    links = [(has_prev, "ctx", p - 1), (has_next, "ctx", p + 1)]
    for d in spans:
        links += [(sends_far(d), "ctx", p + d), (gets_far(d), "ctx", p - d)]
    for j in range(bits):
        pl.semaphore_signal(bar, inc=1, device_id={"section": other(j)[0]}, device_id_type=pl.DeviceIdType.MESH)
    for cond, axis, to in links:
        @pl.when(cond)
        def _(axis=axis, to=to):
            pl.semaphore_signal(bar, inc=1, device_id={axis: to}, device_id_type=pl.DeviceIdType.MESH)
    peers = bits
    for cond, _, _ in links:
        peers = peers + jnp.where(cond, 1, 0)
    pl.semaphore_wait(bar, peers)

    def near_copy(h):
        return copy(kv_ref.at[role, h], seen.at[role, h, pl.ds(0, own)], near_s.at[h], near_r.at[h], "ctx", p + 1)

    def far_copy(h, d):
        return copy(kv_ref.at[role, h, 0], seen.at[role, h, own + index], far_s.at[h, d], far_r.at[h, index],
                    "ctx", p + d)

    def far_arrival(h, n):
        return copy(kv_ref.at[role, h, 0], seen.at[role, h, own + n], far_s.at[h, 0], far_r.at[h, n], "ctx", p)

    def pair_copy(h, half):
        blocks = seen.at[half, h, pl.ds(0, own)]
        return copy(blocks, blocks, pair_s.at[h], pair_r.at[h], "section", mate)

    def farpair_copy(h, n, half):
        block = seen.at[half, h, own + n]
        return copy(block, block, farpair_s.at[h, n], farpair_r.at[h, n], "section", mate)

    def one_copy(h, src_half):
        return copy(parts.at[src_half, h, pl.ds(0, own)], paired.at[h, pl.ds(0, own)],
                    one_s.at[h], one_r.at[h], "section", mate)

    def own_copy(h, src_half):
        return copy(parts.at[src_half, h, pl.ds(own, own)], paired.at[h, pl.ds(own, own)],
                    own_s.at[h], own_r.at[h], "section", mate)

    def farone_copy(h, n, src_half):
        return copy(parts.at[src_half, h, 2 * own + n], paired.at[h, 2 * own + n],
                    farone_s.at[h, n], farone_r.at[h, n], "section", mate)

    def back_copy(h):
        return copy(halves.at[h, pl.ds(0, own)], returned.at[h], back_s.at[h], back_r.at[h], "ctx", p - 1)

    def farback_copy(h, n):
        return copy(halves.at[h, 2 * own + n], farback.at[h, p - n * owner_step], farback_s.at[h, n],
                    farback_r.at[h, p - n * owner_step], "ctx", n * owner_step)

    def farback_arrival(h, d):
        return copy(halves.at[h, 2 * own], farback.at[h, d], farback_s.at[h, 0], farback_r.at[h, d], "ctx", p)

    def two_copy(h, j):
        return copy(totals.at[j, h], swapped.at[j, h], two_s.at[j, h], two_r.at[j, h], "section", other(j)[0])

    def three_copy(h, half):
        return copy(out_ref.at[half, h], out_ref.at[half, h], three_s.at[h], three_r.at[h], "section", mate)

    for h in range(heads):
        @pl.when(has_next)
        def _(h=h):
            near_copy(h).start()
        for d in spans:
            @pl.when(sends_far(d))
            def _(h=h, d=d):
                far_copy(h, d).start()

    @pl.when(jnp.logical_not(has_prev))
    def _():
        seen[:, :, :own] = jnp.zeros_like(seen[:, :, :own])
    for n in range(n_glob):
        @pl.when(p < n * owner_step + 1)
        def _(n=n):
            seen[:, :, own + n] = jnp.zeros_like(seen[:, :, own + n])

    def pass_on(h):
        @pl.when(has_prev)
        def _():
            near_copy(h).wait_recv()
            pair_copy(h, role).start()
        for n in range(n_glob):
            @pl.when(is_far(n))
            def _(n=n):
                far_arrival(h, n).wait_recv()
                farpair_copy(h, n, role).start()

    def arrived(h):
        @pl.when(has_prev)
        def _():
            pair_copy(h, 1 - role).wait_recv()
        for n in range(n_glob):
            @pl.when(is_far(n))
            def _(n=n):
                farpair_copy(h, n, 1 - role).wait_recv()

            @pl.when(is_next(n))
            def _(n=n):
                seen[:, h, own + n] = seen[:, h, 0]

    touched = set()

    def add_to(which):
        def add(slot, part):
            if (which, slot) in touched:
                acc[which, slot] += part
            else:
                acc[which, slot] = part
                touched.add((which, slot))
        return add

    def block_of(which, h):
        def get(slot):
            if slot < own:
                return seen[which, h, slot]
            if slot < 2 * own:
                return kv_ref[which, h, slot - own]
            return seen[which, h, slot - own]
        return get

    def compute(h, rows):
        def spots(i):
            return [pl.ds(i * BLK * lanes + h * group + n, BLK, stride=lanes) for n in range(group)]

        def rows_of(ref, i):
            return jnp.concatenate([ref[at, :] for at in spots(i)], axis=0).astype(jnp.bfloat16)

        def put_att(i, x):
            for n, at in enumerate(spots(i)):
                att_wide[at, :] = x[n * BLK:(n + 1) * BLK]

        def put_dq(i, x):
            for n, at in enumerate(spots(i)):
                dq_ref[at, :] = x[n * BLK:(n + 1) * BLK]

        head_rows(own, n_glob, scale, p * own, band_ref, glob_ref, lambda i: rows_of(q_wide, i), lambda i: rows_of(g_wide, i),
                  block_of(0, h), block_of(1, h), put_att, put_dq, add_to(0), add_to(1), rows)

    def send_parts(h):
        for n in range(n_glob):
            @pl.when(is_next(n))
            def _(n=n):
                acc[:, 0] += acc[:, 2 * own + n]
        parts[:, h] = acc[...].astype(parts.dtype)
        one_copy(h, 1 - role).start()
        for n in range(n_glob):
            @pl.when(is_far(n))
            def _(n=n):
                farone_copy(h, n, 1 - role).start()
        own_copy(h, 1 - role).start()

    def wide(x):
        return x.astype(jnp.float32)

    def send_back(h):
        one_copy(h, role).wait_recv()
        both = pl.ds(0, own)
        halves[h, both] = (wide(parts[role, h, both]) + wide(paired[h, both])).astype(halves.dtype)

        @pl.when(has_prev)
        def _():
            back_copy(h).start()
        for n in range(n_glob):
            @pl.when(is_far(n))
            def _(n=n):
                farone_copy(h, n, role).wait_recv()
                at = 2 * own + n
                halves[h, at] = (wide(parts[role, h, at]) + wide(paired[h, at])).astype(halves.dtype)
                farback_copy(h, n).start()
        own_copy(h, role).wait_recv()
        mine = pl.ds(own, own)
        halves[h, mine] = (wide(parts[role, h, mine]) + wide(paired[h, mine])).astype(halves.dtype)

    def swap(h):
        mine = pl.ds(own, own)
        total = acc_own
        total[...] = wide(halves[h, mine])

        @pl.when(has_next)
        def _():
            back_copy(h).wait_recv()
            total[...] += wide(returned[h])
        for d in spans:
            @pl.when(sends_far(d))
            def _(d=d):
                farback_arrival(h, d).wait_recv()
                total[0] += wide(farback[h, d])
        totals[1, h] = total[...].astype(totals.dtype)
        two_copy(h, 1).start()

    def spread(h):
        for j in range(1, bits):
            two_copy(h, j).wait_recv()
            result = (wide(totals[j, h]) + wide(swapped[j, h])).astype(totals.dtype)
            if j + 1 < bits:
                totals[j + 1, h] = result
                two_copy(h, j + 1).start()
            else:
                out_ref[role, h] = result
        three_copy(h, role).start()

    q_wide[...] = q_ref[...].astype(jnp.float32)
    g_wide[...] = g_ref[...].astype(jnp.float32)
    pass_on(0)

    def step(h, carry):
        @pl.when(h + 1 < heads)
        def _():
            pass_on(h + 1)

        @pl.when(h >= 3)
        def _():
            spread(h - 3)

        @pl.when(jnp.logical_and(h >= 2, h < heads + 2))
        def _():
            swap(h - 2)

        @pl.when(h < heads)
        def _():
            arrived(h)
            compute(h, range(own // 2))

        @pl.when(h == heads)
        def _():
            att_ref[...] = att_wide[...].astype(att_ref.dtype)

        @pl.when(jnp.logical_and(h >= 1, h < heads + 1))
        def _():
            send_back(h - 1)

        @pl.when(h < heads)
        def _():
            compute(h, range(own // 2, own))
            send_parts(h)
        return carry

    lax.fori_loop(0, heads + 3, step, 0)

    def finish(h, carry):
        @pl.when(has_next)
        def _():
            near_copy(h).wait_send()
        for d in spans:
            @pl.when(sends_far(d))
            def _(d=d):
                far_copy(h, d).wait_send()

        @pl.when(has_prev)
        def _():
            pair_copy(h, role).wait_send()
            back_copy(h).wait_send()
        one_copy(h, 1 - role).wait_send()
        own_copy(h, 1 - role).wait_send()
        for n in range(n_glob):
            @pl.when(is_far(n))
            def _(n=n):
                farpair_copy(h, n, role).wait_send()
                farone_copy(h, n, 1 - role).wait_send()
                farback_copy(h, n).wait_send()
        for j in range(1, bits):
            two_copy(h, j).wait_send()
        three_copy(h, role).wait_send()
        three_copy(h, 1 - role).wait_recv()
        for which, ref in enumerate((dkey_ref, dvalue_ref)):
            ref[pl.ds(h, tok, stride=heads), :] = wide(out_ref[which, h]).reshape(tok, dim)
        return carry

    lax.fori_loop(0, heads, finish, 0)


def shards(queries, key_states, value_states, out_grad, band_offsets, global_blocks):
    tok, heads, group, dim = queries.shape
    own = tok // BLK
    ctx_count, sections = lax.axis_size("ctx"), lax.axis_size("section")
    bits = sections.bit_length() - 1
    all_blocks = own * ctx_count
    stride_blocks = all_blocks // NGLOB
    n_glob = global_count(all_blocks, stride_blocks, own)
    slots = 2 * own + n_glob
    flat, narrow = (tok * heads * group, dim), (tok * heads, dim)
    smem, vmem = pl.BlockSpec(memory_space=pltpu.SMEM), pl.BlockSpec(memory_space=pltpu.VMEM)

    def low(*lead):
        return pltpu.VMEM((*lead, BLK, dim), jnp.bfloat16)

    def sems(*dims):
        return [pltpu.SemaphoreType.DMA(dims)] * 2

    att, dq, dkey, dvalue = pl.pallas_call(
        functools.partial(fused_kernel, own, n_glob, stride_blocks // own, ctx_count, bits, dim ** (-0.5), group),
        in_specs=[smem, smem, vmem, vmem, vmem, vmem],
        out_specs=[vmem, vmem, vmem, vmem],
        out_shape=[
            jax.ShapeDtypeStruct(flat, jnp.bfloat16),
            jax.ShapeDtypeStruct(flat, jnp.float32),
            jax.ShapeDtypeStruct(narrow, jnp.float32),
            jax.ShapeDtypeStruct(narrow, jnp.float32),
        ],
        scratch_shapes=[
            pltpu.VMEM(narrow, jnp.float32), low(2, heads, own),
            pltpu.VMEM(flat, jnp.float32), pltpu.VMEM(flat, jnp.float32), pltpu.VMEM(flat, jnp.float32),
            low(2, heads, own),
            low(2, heads, own + n_glob),
            pltpu.VMEM((2, slots, BLK, dim), jnp.float32),
            pltpu.VMEM((own, BLK, dim), jnp.float32),
            low(2, heads, slots), low(heads, slots), low(heads, slots), low(heads, own), low(heads, ctx_count),
            low(bits, heads, own), low(bits, heads, own),
            *sems(heads), pltpu.SemaphoreType.DMA((heads, ctx_count)), pltpu.SemaphoreType.DMA((heads, n_glob)),
            *sems(heads), *sems(heads, n_glob),
            *sems(heads), *sems(heads), *sems(heads, n_glob),
            *sems(heads), pltpu.SemaphoreType.DMA((heads, n_glob)), pltpu.SemaphoreType.DMA((heads, ctx_count)),
            *sems(bits, heads), *sems(heads),
        ],
        compiler_params=pltpu.CompilerParams(
            vmem_limit_bytes=56 * 2**20, collective_id=0, has_side_effects=True),
    )(band_offsets.T, global_blocks.T, queries.reshape(flat), out_grad.reshape(flat),
      key_states.reshape(narrow), value_states.reshape(narrow))
    return (att.reshape(queries.shape), dq.reshape(queries.shape), dkey.reshape(key_states.shape),
            dvalue.reshape(key_states.shape))


def solution(mesh):
    wide, narrow = P("ctx", "tp", "section", None), P("ctx", "tp", None)
    return jax.shard_map(
        shards,
        mesh=mesh,
        in_specs=(wide, narrow, narrow, wide, P(), P()),
        out_specs=(wide, wide, narrow, narrow),
        check_vma=False,
    )
```

```python
import functools

import jax
import jax.numpy as jnp
from jax import lax
from jax.experimental import pallas as pl
from jax.experimental.pallas import tpu as pltpu
from jax.sharding import PartitionSpec as P

BLK = 128
NBAND = 3
NGLOB = 4
REACH = ((1, 2), (3, 4))
LOG2E = 1.4426950408889634
LOW = -1e30


def global_count(all_blocks, stride_blocks, own_blocks):
    return len([n for n in range(NGLOB) if n * stride_blocks < all_blocks - 1 - own_blocks])


def dot_nt(a, b):
    return lax.dot_general(a, b, (((1,), (1,)), ((), ())), preferred_element_type=jnp.float32)


def dot_tn(a, b):
    return lax.dot_general(a, b, (((0,), (0,)), ((), ())), preferred_element_type=jnp.float32)


def dot_nn(a, b):
    return lax.dot_general(a, b, (((1,), (0,)), ((), ())), preferred_element_type=jnp.float32)


def head_rows(own_blocks, n_glob, scale, row_base, band_ref, glob_ref, q_of, g_of, key_of, value_of,
              put_att, put_dq, add_key, add_value, rows):
    for i in rows:
        row = row_base + i
        offs = [band_ref[1 + m, row] for m in range(NBAND - 1)]
        chosen = [glob_ref[n, row] for n in range(n_glob)]
        q, g = q_of(i), g_of(i)

        def selected(block_of):
            parts = [block_of(own_blocks + i)]
            for m in range(NBAND - 1):
                near, far = REACH[m]
                parts.append(jnp.where(offs[m] == near, block_of(own_blocks + i - near),
                                       block_of(own_blocks + i - far)))
            for n in range(n_glob):
                parts.append(block_of(2 * own_blocks + n))
            return jnp.concatenate(parts, axis=0)

        keys, values = selected(key_of), selected(value_of)
        scores = dot_nt(keys, q)
        width = scores.shape[1]
        key_pos = lax.broadcasted_iota(jnp.int32, (BLK, width), 0)
        query_pos = lax.broadcasted_iota(jnp.int32, (BLK, width), 1) % BLK
        usable = [o >= 0 for o in offs] + [c >= 0 for c in chosen]
        pieces = [jnp.where(key_pos <= query_pos, scores[:BLK], LOW)]
        for n, ok in enumerate(usable):
            pieces.append(scores[(n + 1) * BLK:(n + 2) * BLK] + jnp.where(ok, 0.0, LOW))
        scores = jnp.concatenate(pieces, axis=0)
        top = jnp.max(scores, axis=0, keepdims=True)
        probs = jnp.exp2((scores - top) * (scale * LOG2E))
        weights = probs * (1.0 / jnp.sum(probs, axis=0, keepdims=True))
        low = weights.astype(jnp.bfloat16)
        att = dot_tn(values, low).astype(jnp.bfloat16).astype(jnp.float32)
        put_att(i, att.T)
        dots = jnp.sum(g.astype(jnp.float32).T * att, axis=0, keepdims=True)
        ds = (weights * (dot_nt(values, g) - dots)).astype(jnp.bfloat16)
        put_dq(i, (dot_tn(keys, ds) * scale).T)
        dk, dv = dot_nn(ds, q) * scale, dot_nn(low, g)
        for part, add in ((dk, add_key), (dv, add_value)):
            add(own_blocks + i, part[:BLK])
            for m in range(NBAND - 1):
                piece = part[(m + 1) * BLK:(m + 2) * BLK]
                for off in REACH[m]:
                    add(own_blocks + i - off, jnp.where(offs[m] == off, piece, 0.0))
            for n in range(n_glob):
                at = (NBAND + n) * BLK
                add(2 * own_blocks + n, part[at:at + BLK])


def fused_kernel(own, n_glob, owner_step, ctx_count, bits, scale, group, band_ref, glob_ref, q_ref, g_ref,
                 key_ref, value_ref, att_ref, dq_ref, dkey_ref, dvalue_ref,
                 kv_wide, kv_ref, q_wide, g_wide, att_wide, out_ref, seen, acc, acc_own, parts, paired, halves, returned, farback, totals, swapped,
                 near_s, near_r, far_s, far_r, pair_s, pair_r, farpair_s, farpair_r,
                 one_s, one_r, own_s, own_r, farone_s, farone_r, back_s, back_r, farback_s, farback_r,
                 two_s, two_r, three_s, three_r):
    heads, dim = kv_ref.shape[1], kv_ref.shape[-1]
    tok, lanes = own * BLK, heads * group

    for which, ref in enumerate((key_ref, value_ref)):
        kv_wide[...] = ref[...].astype(jnp.float32)
        for h in range(heads):
            kv_ref[which, h] = kv_wide[pl.ds(h, tok, stride=heads), :].astype(kv_ref.dtype).reshape(own, BLK, dim)
    p, s, parity = lax.axis_index("ctx"), lax.axis_index("section"), lax.axis_index("tp") % 2

    def other(j):
        bit = (1 << (j % bits)) * (1 - parity) + (1 << ((j + 1) % bits)) * parity
        side = (s // bit) % 2
        return s + bit * (1 - 2 * side), side

    mate, role = other(0)
    has_prev, has_next = p > 0, p < ctx_count - 1
    index = p // owner_step

    def owns(at):
        return jnp.logical_and(at % owner_step == 0, at // owner_step < n_glob)

    def sends_far(d):
        return jnp.logical_and(owns(p), p + d < ctx_count)

    def gets_far(d):
        return jnp.logical_and(p - d >= 0, owns(p - d + (p - d < 0) * ctx_count * owner_step))

    spans = range(2, ctx_count)

    def is_far(n):
        return p >= n * owner_step + 2

    def is_next(n):
        return p == n * owner_step + 1

    def copy(src, dst, ss, rs, axis, to):
        return pltpu.make_async_remote_copy(src_ref=src, dst_ref=dst, send_sem=ss, recv_sem=rs,
                                            device_id={axis: to}, device_id_type=pl.DeviceIdType.MESH)

    bar = pltpu.get_barrier_semaphore()
    links = [(has_prev, "ctx", p - 1), (has_next, "ctx", p + 1)]
    for d in spans:
        links += [(sends_far(d), "ctx", p + d), (gets_far(d), "ctx", p - d)]
    for j in range(bits):
        pl.semaphore_signal(bar, inc=1, device_id={"section": other(j)[0]}, device_id_type=pl.DeviceIdType.MESH)
    for cond, axis, to in links:
        @pl.when(cond)
        def _(axis=axis, to=to):
            pl.semaphore_signal(bar, inc=1, device_id={axis: to}, device_id_type=pl.DeviceIdType.MESH)
    peers = bits
    for cond, _, _ in links:
        peers = peers + jnp.where(cond, 1, 0)
    pl.semaphore_wait(bar, peers)

    def near_copy(h):
        return copy(kv_ref.at[role, h], seen.at[role, h, pl.ds(0, own)], near_s.at[h], near_r.at[h], "ctx", p + 1)

    def far_copy(h, d):
        return copy(kv_ref.at[role, h, 0], seen.at[role, h, own + index], far_s.at[h, d], far_r.at[h, index],
                    "ctx", p + d)

    def far_arrival(h, n):
        return copy(kv_ref.at[role, h, 0], seen.at[role, h, own + n], far_s.at[h, 0], far_r.at[h, n], "ctx", p)

    def pair_copy(h, half):
        blocks = seen.at[half, h, pl.ds(0, own)]
        return copy(blocks, blocks, pair_s.at[h], pair_r.at[h], "section", mate)

    def farpair_copy(h, n, half):
        block = seen.at[half, h, own + n]
        return copy(block, block, farpair_s.at[h, n], farpair_r.at[h, n], "section", mate)

    def one_copy(h, src_half):
        return copy(parts.at[src_half, h, pl.ds(0, own)], paired.at[h, pl.ds(0, own)],
                    one_s.at[h], one_r.at[h], "section", mate)

    def own_copy(h, src_half):
        return copy(parts.at[src_half, h, pl.ds(own, own)], paired.at[h, pl.ds(own, own)],
                    own_s.at[h], own_r.at[h], "section", mate)

    def farone_copy(h, n, src_half):
        return copy(parts.at[src_half, h, 2 * own + n], paired.at[h, 2 * own + n],
                    farone_s.at[h, n], farone_r.at[h, n], "section", mate)

    def back_copy(h):
        return copy(halves.at[h, pl.ds(0, own)], returned.at[h], back_s.at[h], back_r.at[h], "ctx", p - 1)

    def farback_copy(h, n):
        return copy(halves.at[h, 2 * own + n], farback.at[h, p - n * owner_step], farback_s.at[h, n],
                    farback_r.at[h, p - n * owner_step], "ctx", n * owner_step)

    def farback_arrival(h, d):
        return copy(halves.at[h, 2 * own], farback.at[h, d], farback_s.at[h, 0], farback_r.at[h, d], "ctx", p)

    def two_copy(h, j):
        return copy(totals.at[j, h], swapped.at[j, h], two_s.at[j, h], two_r.at[j, h], "section", other(j)[0])

    def three_copy(h, half):
        return copy(out_ref.at[half, h], out_ref.at[half, h], three_s.at[h], three_r.at[h], "section", mate)

    for h in range(heads):
        @pl.when(has_next)
        def _(h=h):
            near_copy(h).start()
        for d in spans:
            @pl.when(sends_far(d))
            def _(h=h, d=d):
                far_copy(h, d).start()

    @pl.when(jnp.logical_not(has_prev))
    def _():
        seen[:, :, :own] = jnp.zeros_like(seen[:, :, :own])
    for n in range(n_glob):
        @pl.when(p < n * owner_step + 1)
        def _(n=n):
            seen[:, :, own + n] = jnp.zeros_like(seen[:, :, own + n])

    def pass_on(h):
        @pl.when(has_prev)
        def _():
            near_copy(h).wait_recv()
            pair_copy(h, role).start()
        for n in range(n_glob):
            @pl.when(is_far(n))
            def _(n=n):
                far_arrival(h, n).wait_recv()
                farpair_copy(h, n, role).start()

    def arrived(h):
        @pl.when(has_prev)
        def _():
            pair_copy(h, 1 - role).wait_recv()
        for n in range(n_glob):
            @pl.when(is_far(n))
            def _(n=n):
                farpair_copy(h, n, 1 - role).wait_recv()

            @pl.when(is_next(n))
            def _(n=n):
                seen[:, h, own + n] = seen[:, h, 0]

    touched = set()

    def add_to(which):
        def add(slot, part):
            if (which, slot) in touched:
                acc[which, slot] += part
            else:
                acc[which, slot] = part
                touched.add((which, slot))
        return add

    def block_of(which, h):
        def get(slot):
            if slot < own:
                return seen[which, h, slot]
            if slot < 2 * own:
                return kv_ref[which, h, slot - own]
            return seen[which, h, slot - own]
        return get

    def compute(h, rows):
        def spots(i):
            return [pl.ds(i * BLK * lanes + h * group + n, BLK, stride=lanes) for n in range(group)]

        def rows_of(ref, i):
            return jnp.concatenate([ref[at, :] for at in spots(i)], axis=0).astype(jnp.bfloat16)

        def put_att(i, x):
            for n, at in enumerate(spots(i)):
                att_wide[at, :] = x[n * BLK:(n + 1) * BLK]

        def put_dq(i, x):
            for n, at in enumerate(spots(i)):
                dq_ref[at, :] = x[n * BLK:(n + 1) * BLK]

        head_rows(own, n_glob, scale, p * own, band_ref, glob_ref, lambda i: rows_of(q_wide, i), lambda i: rows_of(g_wide, i),
                  block_of(0, h), block_of(1, h), put_att, put_dq, add_to(0), add_to(1), rows)

    def send_parts(h):
        for n in range(n_glob):
            @pl.when(is_next(n))
            def _(n=n):
                acc[:, 0] += acc[:, 2 * own + n]
        parts[:, h] = acc[...].astype(parts.dtype)
        one_copy(h, 1 - role).start()
        for n in range(n_glob):
            @pl.when(is_far(n))
            def _(n=n):
                farone_copy(h, n, 1 - role).start()
        own_copy(h, 1 - role).start()

    def wide(x):
        return x.astype(jnp.float32)

    def send_back(h):
        one_copy(h, role).wait_recv()
        both = pl.ds(0, own)
        halves[h, both] = (wide(parts[role, h, both]) + wide(paired[h, both])).astype(halves.dtype)

        @pl.when(has_prev)
        def _():
            back_copy(h).start()
        for n in range(n_glob):
            @pl.when(is_far(n))
            def _(n=n):
                farone_copy(h, n, role).wait_recv()
                at = 2 * own + n
                halves[h, at] = (wide(parts[role, h, at]) + wide(paired[h, at])).astype(halves.dtype)
                farback_copy(h, n).start()
        own_copy(h, role).wait_recv()
        mine = pl.ds(own, own)
        halves[h, mine] = (wide(parts[role, h, mine]) + wide(paired[h, mine])).astype(halves.dtype)

    def swap(h):
        mine = pl.ds(own, own)
        total = acc_own
        total[...] = wide(halves[h, mine])

        @pl.when(has_next)
        def _():
            back_copy(h).wait_recv()
            total[...] += wide(returned[h])
        for d in spans:
            @pl.when(sends_far(d))
            def _(d=d):
                farback_arrival(h, d).wait_recv()
                total[0] += wide(farback[h, d])
        totals[1, h] = total[...].astype(totals.dtype)
        two_copy(h, 1).start()

    def spread(h):
        for j in range(1, bits):
            two_copy(h, j).wait_recv()
            result = (wide(totals[j, h]) + wide(swapped[j, h])).astype(totals.dtype)
            if j + 1 < bits:
                totals[j + 1, h] = result
                two_copy(h, j + 1).start()
            else:
                out_ref[role, h] = result
        three_copy(h, role).start()

    q_wide[...] = q_ref[...].astype(jnp.float32)
    g_wide[...] = g_ref[...].astype(jnp.float32)
    pass_on(0)

    def step(h, carry):
        @pl.when(h >= 3)
        def _():
            spread(h - 3)

        @pl.when(jnp.logical_and(h >= 2, h < heads + 2))
        def _():
            swap(h - 2)

        @pl.when(h < heads)
        def _():
            arrived(h)
            compute(h, range(own // 2))

        @pl.when(h + 1 < heads)
        def _():
            pass_on(h + 1)

        @pl.when(h == heads)
        def _():
            att_ref[...] = att_wide[...].astype(att_ref.dtype)

        @pl.when(jnp.logical_and(h >= 1, h < heads + 1))
        def _():
            send_back(h - 1)

        @pl.when(h < heads)
        def _():
            compute(h, range(own // 2, own))
            send_parts(h)
        return carry

    lax.fori_loop(0, heads + 3, step, 0)

    def finish(h, carry):
        @pl.when(has_next)
        def _():
            near_copy(h).wait_send()
        for d in spans:
            @pl.when(sends_far(d))
            def _(d=d):
                far_copy(h, d).wait_send()

        @pl.when(has_prev)
        def _():
            pair_copy(h, role).wait_send()
            back_copy(h).wait_send()
        one_copy(h, 1 - role).wait_send()
        own_copy(h, 1 - role).wait_send()
        for n in range(n_glob):
            @pl.when(is_far(n))
            def _(n=n):
                farpair_copy(h, n, role).wait_send()
                farone_copy(h, n, 1 - role).wait_send()
                farback_copy(h, n).wait_send()
        for j in range(1, bits):
            two_copy(h, j).wait_send()
        three_copy(h, role).wait_send()
        three_copy(h, 1 - role).wait_recv()
        for which, ref in enumerate((dkey_ref, dvalue_ref)):
            ref[pl.ds(h, tok, stride=heads), :] = wide(out_ref[which, h]).reshape(tok, dim)
        return carry

    lax.fori_loop(0, heads, finish, 0)


def shards(queries, key_states, value_states, out_grad, band_offsets, global_blocks):
    tok, heads, group, dim = queries.shape
    own = tok // BLK
    ctx_count, sections = lax.axis_size("ctx"), lax.axis_size("section")
    bits = sections.bit_length() - 1
    all_blocks = own * ctx_count
    stride_blocks = all_blocks // NGLOB
    n_glob = global_count(all_blocks, stride_blocks, own)
    slots = 2 * own + n_glob
    flat, narrow = (tok * heads * group, dim), (tok * heads, dim)
    smem, vmem = pl.BlockSpec(memory_space=pltpu.SMEM), pl.BlockSpec(memory_space=pltpu.VMEM)

    def low(*lead):
        return pltpu.VMEM((*lead, BLK, dim), jnp.bfloat16)

    def sems(*dims):
        return [pltpu.SemaphoreType.DMA(dims)] * 2

    att, dq, dkey, dvalue = pl.pallas_call(
        functools.partial(fused_kernel, own, n_glob, stride_blocks // own, ctx_count, bits, dim ** (-0.5), group),
        in_specs=[smem, smem, vmem, vmem, vmem, vmem],
        out_specs=[vmem, vmem, vmem, vmem],
        out_shape=[
            jax.ShapeDtypeStruct(flat, jnp.bfloat16),
            jax.ShapeDtypeStruct(flat, jnp.float32),
            jax.ShapeDtypeStruct(narrow, jnp.float32),
            jax.ShapeDtypeStruct(narrow, jnp.float32),
        ],
        scratch_shapes=[
            pltpu.VMEM(narrow, jnp.float32), low(2, heads, own),
            pltpu.VMEM(flat, jnp.float32), pltpu.VMEM(flat, jnp.float32), pltpu.VMEM(flat, jnp.float32),
            low(2, heads, own),
            low(2, heads, own + n_glob),
            pltpu.VMEM((2, slots, BLK, dim), jnp.float32),
            pltpu.VMEM((own, BLK, dim), jnp.float32),
            low(2, heads, slots), low(heads, slots), low(heads, slots), low(heads, own), low(heads, ctx_count),
            low(bits, heads, own), low(bits, heads, own),
            *sems(heads), pltpu.SemaphoreType.DMA((heads, ctx_count)), pltpu.SemaphoreType.DMA((heads, n_glob)),
            *sems(heads), *sems(heads, n_glob),
            *sems(heads), *sems(heads), *sems(heads, n_glob),
            *sems(heads), pltpu.SemaphoreType.DMA((heads, n_glob)), pltpu.SemaphoreType.DMA((heads, ctx_count)),
            *sems(bits, heads), *sems(heads),
        ],
        compiler_params=pltpu.CompilerParams(
            vmem_limit_bytes=40 * 2**20, collective_id=0, has_side_effects=True),
    )(band_offsets.T, global_blocks.T, queries.reshape(flat), out_grad.reshape(flat),
      key_states.reshape(narrow), value_states.reshape(narrow))
    return (att.reshape(queries.shape), dq.reshape(queries.shape), dkey.reshape(key_states.shape),
            dvalue.reshape(key_states.shape))


def solution(mesh):
    wide, narrow = P("ctx", "tp", "section", None), P("ctx", "tp", None)
    return jax.shard_map(
        shards,
        mesh=mesh,
        in_specs=(wide, narrow, narrow, wide, P(), P()),
        out_specs=(wide, wide, narrow, narrow),
        check_vma=False,
    )
```
